32 devices in a mesh: groups: 2 (over x), seq: 4 (over y, core), head: 4 (over z).
Axes of the slice: x: 2, y: 2, z: 4, core: 2. Of those that a mesh axis runs over, the one named last changes fastest.
Arguments:
- mixer_input: bfloat16 [1024, 16384], P(('groups', 'seq'), 'head'), parts along dimension 0, may hold values from -6 to 6
- state_input: bfloat16 [1024, 1024], P(('groups', 'seq'), 'head'), parts along dimension 0, may hold values from -0.5 to 0.5
- state_output: bfloat16 [1024, 1024], P(('groups', 'seq'), 'head'), parts along dimension 0, may hold values from -0.5 to 0.5
- log_decay: float32 [256, 1024], P('head', ('groups', 'seq')), parts along dimension 1, may hold values from -1 to 0, as said below
- step_size: float32 [256, 1024], P('head', ('groups', 'seq')), parts along dimension 1, may hold values from 0.05 to 0.5
- skip_gain: float32 [256], P('head'), may hold values from 0.5 to 1.5
- residual: bfloat16 [1024, 8192], P(('groups', 'seq'), 'head'), parts along dimension 0, may hold values from -256 to 256, as said below
- out_proj: bfloat16 [16384, 8192], P('head', 'seq'), may hold values from -0.046875 to 0.046875
- norm_gain: float32 [8192], P('seq'), may hold values from 0.1 to 1.9
- lens_weight: bfloat16 [8192, 65536], P('seq', 'head'), may hold values from -32 to 32
- probe_position: int32 [256], P(('groups', 'seq')), parts along dimension 0, may hold values from -1 to 127, as said below
- probe_layer: int32 [256], P(('groups', 'seq')), parts along dimension 0, may hold values from 0 to 1
Outputs:
- mixer_out: bfloat16 [1024, 16384], P(('groups', 'seq'), 'head'), parts along dimension 0
- lens_logprobs: float32 [256, 65536], P(('groups', 'seq'), 'head'), parts along dimension 0
The draws below stay inside these ranges and needn't reach their ends.
There are 2 independent parts, one for each index of `groups`. The reference program is written for one: setup_inputs(seed, part) draws one part's arguments, and reference() takes and returns one part's arrays. A program takes and returns all parts, laid end to end along the dimension named above; an argument that names none is the same for every part. Nothing has to cross between parts.
Inputs may be any that keep to these rules, and one draw needn't show every extreme that they name: `log_decay`: every value is negative. `residual`: the entries of one row of every sequence shard are of mixed scales. `probe_position`: in each shard the live slots come first and the rest hold -1; some shard has all 32 slots live.
All inputs are finite; a program needn't handle non-finite values.
Results may differ from the reference program's by a relative error of at most 0.0054.
Values may be sent and summed in bfloat16 or wider, within the bound.
A program may use at most 192 MiB of HBM per device.

```python
import math
from functools import partial
import jax
import jax.numpy as jnp
from jax import lax

MIXER_HEADS = 256
HEAD_DIM = 64
SSM_GROUPS = 8
STATE = 128
WIDTH = 8192
VOCAB = 65536
BLOCK = 128
TOK_DEV = 128
PROBE_CAP = 32
INNER = 16384
PROMPT_LENGTH = 512
PROBES = 128


def draw_log_decay(key, part):
    key_pick = jax.random.fold_in(key, 101)
    key_slow = jax.random.fold_in(key, 102)
    key_fast = jax.random.fold_in(key, 103)
    key_jitter = jax.random.fold_in(key, 104)
    key_location = jax.random.fold_in(key, 105)
    key_spike = jax.random.fold_in(key, 106)
    pick = jax.random.randint(key_pick, (MIXER_HEADS,), 0, 8)
    is_fast = pick < 4
    slow_rate = jnp.exp(jax.random.uniform(key_slow, (MIXER_HEADS,), minval=math.log(0.1), maxval=math.log(0.6))) / PROMPT_LENGTH
    fast_rate = jnp.exp(jax.random.uniform(key_fast, (MIXER_HEADS,), minval=math.log(1.0 / 50.0), maxval=math.log(1.0 / 30.0)))
    decay_speed = jnp.where(is_fast, fast_rate, slow_rate)
    small_noise = jnp.exp(jax.random.uniform(key_jitter, (MIXER_HEADS, PROMPT_LENGTH), minval=math.log(0.5), maxval=math.log(2.0)))
    spike_position = jax.random.randint(key_location, (3,), 0, PROMPT_LENGTH)
    spike_match = jnp.any(jnp.arange(PROMPT_LENGTH)[:, None] == spike_position[None, :], axis=1)
    spike_amount = jax.random.uniform(key_spike, (MIXER_HEADS, PROMPT_LENGTH), minval=0.22, maxval=0.5)
    value_entries = -(decay_speed[:, None] * small_noise) - jnp.where(spike_match[None, :], spike_amount, 0.0)
    return jnp.clip(value_entries, -1.0, 0.0).astype(jnp.float32)


def draw_residual(key, part):
    key_rows = jax.random.fold_in(key, 201)
    key_cols = jax.random.fold_in(key, 202)
    key_noise = jax.random.fold_in(key, 203)
    row_scale = 10.0 ** jax.random.uniform(key_rows, (PROMPT_LENGTH, 1), minval=0.0, maxval=1.0)
    column = jnp.arange(WIDTH).astype(jnp.float32) / WIDTH
    col_scale = 3.0 ** column * 10.0 ** jax.random.uniform(key_cols, (WIDTH,), minval=0.0, maxval=1.0)
    noise = jax.random.normal(key_noise, (PROMPT_LENGTH, WIDTH))
    value_entries = noise * row_scale * col_scale[None, :] / 10.0
    return jnp.clip(value_entries, -256.0, 256.0).astype(jnp.bfloat16)


def draw_lens_weight(key, part):
    key_base = jax.random.fold_in(key, 301)
    column = jnp.arange(VOCAB)
    column_tilt = 1.0 + 0.12 * column.astype(jnp.float32) / VOCAB
    weights = jax.random.normal(key_base, (WIDTH, VOCAB)) * (3.0 / math.sqrt(WIDTH)) * column_tilt[None, :]
    return jnp.clip(weights, -32.0, 32.0).astype(jnp.bfloat16)


def draw_probe_position(key, part):
    key_counts = jax.random.fold_in(key, 401)
    key_full = jax.random.fold_in(key, 402)
    key_places = jax.random.fold_in(key, 403)
    shards = PROBES // PROBE_CAP
    counts = jax.random.randint(key_counts, (shards,), PROBE_CAP // 4, PROBE_CAP + 1)
    fullest = jax.random.randint(key_full, (), 0, shards)
    shard_order = jnp.arange(shards)
    counts = jnp.where(shard_order == fullest, PROBE_CAP, counts)
    counts = jnp.where(shard_order == (fullest + 1) % shards, PROBE_CAP // 4, counts)
    places = jax.random.randint(key_places, (shards, PROBE_CAP), 0, TOK_DEV)
    slot_order = jnp.arange(PROBE_CAP)[None, :]
    places = jnp.where((shard_order[:, None] == fullest) & (slot_order == 0), TOK_DEV - 1, places)
    value_entries = jnp.where(slot_order < counts[:, None], places, -1)
    return value_entries.reshape(PROBES).astype(jnp.int32)


def touch_ends(entries, rng, low, largest):
    place = [jax.random.randint(jax.random.fold_in(rng, axis), (), 0, length) for axis, length in enumerate(entries.shape)]
    longest = entries.shape.index(max(entries.shape))
    beside = place[:longest] + [(place[longest] + 1) % entries.shape[longest]] + place[longest + 1:]
    return entries.at[tuple(place)].set(low).at[tuple(beside)].set(largest)


def block_scale(rng, shape, cuts, least, high):
    def one(position, blocks):
        steps = jax.random.uniform(jax.random.fold_in(jax.random.fold_in(rng, 6), position), (blocks,), jnp.float32, least / len(cuts), high / len(cuts))
        return jnp.repeat(jnp.exp(steps), shape[position] // blocks).reshape((-1,) + (1,) * (len(shape) - position - 1))

    loudness = one(*cuts[0])
    for cut in cuts[1:]:
        loudness = loudness * one(*cut)
    return loudness


def gaussian(rng, extent, width, limit, cuts=(), kind=jnp.bfloat16):
    drawn = jax.random.normal(rng, extent, jnp.float32) * width
    if len(cuts) > 0:
        drawn = block_scale(rng, extent, cuts, -0.22, 0.18) * drawn
    return jnp.clip(drawn, min=-limit, max=limit).astype(kind)


def setup_inputs(seed: int = 0, part: int = 0) -> dict:
    arg_keys = jax.random.split(jax.random.key(seed), 13)
    part_splits = jax.random.split(jax.random.fold_in(arg_keys[12], part), 13)
    return {
        "mixer_input": gaussian(part_splits[0], (PROMPT_LENGTH, INNER), 1.0, 6.0, ((0, 4), (1, 4))),
        "state_input": gaussian(part_splits[1], (PROMPT_LENGTH, SSM_GROUPS * STATE), STATE ** -0.5, 0.5, ((0, 4), (1, 4))),
        "state_output": gaussian(part_splits[2], (PROMPT_LENGTH, SSM_GROUPS * STATE), STATE ** -0.5, 0.5, ((0, 4), (1, 4))),
        "log_decay": draw_log_decay(jax.random.fold_in(jax.random.fold_in(arg_keys[12], part), 71), part),
        "step_size": jnp.clip(jnp.exp(math.log(0.5) - 2.3025851 * jax.random.uniform(part_splits[4], (MIXER_HEADS, PROMPT_LENGTH), jnp.float32) ** block_scale(part_splits[4], (MIXER_HEADS, PROMPT_LENGTH), ((0, 4), (1, 4)), -0.2, 0.2)), 0.05, 0.5),
        "skip_gain": jnp.clip(0.5 + 1.0 * jax.random.uniform(arg_keys[5], (MIXER_HEADS,), jnp.float32) ** block_scale(arg_keys[5], (MIXER_HEADS,), ((0, 4),), -0.2, 0.2), 0.5, 1.5),
        "residual": draw_residual(jax.random.fold_in(jax.random.fold_in(arg_keys[12], part), 71), part),
        "out_proj": gaussian(arg_keys[7], (INNER, WIDTH), INNER ** -0.5, 0.046875, ((0, 4), (1, 4))),
        "norm_gain": jnp.clip(1.0 + 0.18 * jax.random.normal(arg_keys[8], (WIDTH,), jnp.float32), 0.1, 1.9),
        "lens_weight": draw_lens_weight(jax.random.fold_in(arg_keys[12], 71), part),
        "probe_position": draw_probe_position(jax.random.fold_in(jax.random.fold_in(arg_keys[12], part), 71), part),
        "probe_layer": touch_ends(jax.random.randint(part_splits[11], (PROBES,), 0, 2), jax.random.fold_in(part_splits[11], 1), 0, 1).astype(jnp.int32),
    }


precise = lax.Precision.HIGHEST
epsilon = 1e-05

def advance(skip_pair, running_pair, pieces):
    ssm_state, offset = running_pair
    block_input, block_write, block_read, block_decay, block_step = pieces
    input_wide = block_input.astype(jnp.float32)
    write_wide = block_write.astype(jnp.float32)
    read_wide = block_read.astype(jnp.float32)
    causal = jnp.arange(BLOCK)[:, None] >= jnp.arange(BLOCK)[None, :]
    running = jnp.cumsum(block_decay, axis=2)
    scores = jnp.einsum('tgn,ugn->gtu', read_wide, write_wide, precision=precise)
    decay_gap = running[..., :, None] - running[..., None, :]
    weights = jnp.where(causal, jnp.exp(jnp.where(causal, decay_gap, 0.0)), 0.0)
    weights = weights * block_step[..., None, :] * scores[:, None]
    within = jnp.einsum('gjtu,ugjp->tgjp', weights, input_wide, precision=precise)
    across = jnp.einsum('gjpn,tgn->tgjp', ssm_state, read_wide, precision=precise)
    across = across * jnp.exp(running).transpose(2, 0, 1)[..., None]
    to_end = jnp.exp(running[..., -1:] - running) * block_step
    new_state = jnp.exp(running[..., -1])[..., None, None] * ssm_state
    new_state = new_state + jnp.einsum('gju,ugjp,ugn->gjpn', to_end, input_wide, write_wide, precision=precise)
    result = within + across + skip_pair[None, :, :, None] * input_wide
    return ((new_state, offset + running[..., -1]), result)

def mixer(mixer_input, state_input, state_output, log_decay, step_size, skip_gain):
    per_group = MIXER_HEADS // SSM_GROUPS
    blocks = PROMPT_LENGTH // BLOCK
    block_inputs = mixer_input.reshape(blocks, BLOCK, SSM_GROUPS, per_group, HEAD_DIM)
    block_writes = state_input.reshape(blocks, BLOCK, SSM_GROUPS, STATE)
    block_reads = state_output.reshape(blocks, BLOCK, SSM_GROUPS, STATE)
    block_decays = log_decay.reshape(SSM_GROUPS, per_group, blocks, BLOCK).transpose(2, 0, 1, 3)
    block_steps = step_size.reshape(SSM_GROUPS, per_group, blocks, BLOCK).transpose(2, 0, 1, 3)
    skip_pair = skip_gain.reshape(SSM_GROUPS, per_group)
    start_state = jnp.zeros((SSM_GROUPS, per_group, HEAD_DIM, STATE), jnp.float32)
    start_offset = jnp.zeros((SSM_GROUPS, per_group), jnp.float32)
    _, outputs = lax.scan(partial(advance, skip_pair), (start_state, start_offset), (block_inputs, block_writes, block_reads, block_decays, block_steps))
    return outputs.reshape(PROMPT_LENGTH, MIXER_HEADS * HEAD_DIM)

def reference(mixer_input, state_input, state_output, log_decay, step_size, skip_gain, residual, out_proj, norm_gain, lens_weight, probe_position, probe_layer):
    mixed = mixer(mixer_input, state_input, state_output, log_decay, step_size, skip_gain)
    mixer_out = mixed.astype(jnp.bfloat16)
    shard_of = (jnp.arange(PROBES) // PROBE_CAP).astype(jnp.int32)
    is_live = probe_position >= 0
    token = (shard_of * TOK_DEV + jnp.maximum(probe_position, 0)).astype(jnp.int32)
    layer_out = jnp.dot(mixer_out[token], out_proj, preferred_element_type=jnp.float32)
    picked = residual[token].astype(jnp.float32) + probe_layer.astype(jnp.float32)[:, None] * layer_out
    inverse_rms = lax.rsqrt(lax.optimization_barrier(jnp.sum(picked * picked, axis=1, keepdims=True)) / WIDTH + epsilon)
    normed = jnp.where(is_live[:, None], picked * inverse_rms * norm_gain[None, :], 0.0).astype(jnp.bfloat16)
    logits = jnp.dot(normed, lens_weight, preferred_element_type=jnp.float32)
    highest = lax.optimization_barrier(jnp.max(logits, axis=1, keepdims=True))
    exp_total = lax.optimization_barrier(jnp.sum(jnp.exp(logits - highest), axis=1, keepdims=True))
    lens_logprobs = logits - highest - jnp.log(exp_total)
    return (mixer_out, lens_logprobs)
```

```python
from functools import partial

import jax
import jax.numpy as jnp
from jax import lax
from jax.experimental import pallas as pl
from jax.experimental.pallas import tpu as pltpu
from jax.sharding import PartitionSpec as P

STATE = 128
epsilon = 1e-05
MESH = pl.DeviceIdType.MESH
VMEM = pl.BlockSpec(memory_space=pltpu.VMEM)
ANY = pl.BlockSpec(memory_space=pl.ANY)
bf16 = jnp.bfloat16
f32 = jnp.float32


def remote(src, dst, send, recv, **to):
    return pltpu.make_async_remote_copy(
        src_ref=src, dst_ref=dst, send_sem=send, recv_sem=recv, device_id=to, device_id_type=MESH
    )


def split(value, parts):
    pieces = []
    for _ in range(parts):
        piece = value.astype(bf16)
        pieces.append(piece)
        value = value - piece.astype(f32)
    return pieces


def dot(a, b, over=(1, 0)):
    return lax.dot_general(a, b, (((over[0],), (over[1],)), ((), ())), preferred_element_type=f32)


def iota(shape, axis):
    return lax.broadcasted_iota(jnp.int32, shape, axis)


def lens_kernel(
    ns, nh, x_hbm, write_hbm, read_hbm, decay_ref, step_ref, skip_ref, residual_hbm, pos_ref, layer_ref,
    gain_ref, proj_hbm, lens_hbm, out_ref, logits_hbm, lse_ref,
    x_ref, write_ref, read_ref, residual_ref, isem, logits_ref, osem,
    runs, runs_t, ends_t, grown_t, scores, loc, wbuf, drow, cr, cs, res_ref,
    gat, resbuf, projv, wslots, prodf, sright, sleft, rright, rleft, lhs, ssb, ssr, kbuf, sbuf, rbuf, s2b, s2r, stats, statr,
    csem, crem, wsem, psem, gs, gr, rs, rr, ssr_, srr_, ssl, srl, sqs, sqr, as_, ar, bs, br, hs, hr,
):
    s, h = lax.axis_index("seq"), lax.axis_index("head")
    ny, ratio = ns // 2, ns // nh
    y, c = s // 2, lax.rem(s, 2)
    partner = y * 2 + 1 - c
    probes, rows = res_ref.shape[0], gat.shape[1]
    chunks, wide = gat.shape[0], gat.shape[2]
    width = projv.shape[1]
    nct, tile_w = sright.shape[0], sright.shape[2]
    slots, tile_v = wslots.shape[0], wslots.shape[2]
    tiles = lens_hbm.shape[1] // tile_v
    half = ny * probes

    def block(i):
        return pl.ds(pl.multiple_of(i * probes, probes), probes)

    def weights(t):
        cols = pl.ds(pl.multiple_of(t * tile_v, tile_v), tile_v)
        slot = lax.rem(t, slots)
        return pltpu.make_async_copy(lens_hbm.at[:, cols], wslots.at[slot], wsem.at[slot])

    loads = [
        pltpu.make_async_copy(src, dst, isem.at[i])
        for i, (src, dst) in enumerate(
            ((write_hbm, write_ref), (read_hbm, read_ref), (x_hbm, x_ref), (residual_hbm, residual_ref))
        )
    ]
    for load in loads:
        load.start()
    proj_copy = pltpu.make_async_copy(proj_hbm, projv, psem)

    barrier = pltpu.get_barrier_semaphore()
    for d in range(1, ns):
        pl.semaphore_signal(barrier, inc=1, device_id={"seq": lax.rem(s + d, ns)}, device_id_type=MESH)
    for d in range(1, nh):
        pl.semaphore_signal(barrier, inc=1, device_id={"head": lax.rem(h + d, nh)}, device_id_type=MESH)
    pl.semaphore_wait(barrier, ns + nh - 2)
    for load in loads:
        load.wait()
    proj_copy.start()
    for t in range(min(slots, tiles)):
        weights(t).start()

    def at_y(d):
        return lax.rem(y + d + ny, ny) * 2

    tokens, heads = x_ref.shape[0], decay_ref.shape[0]
    size = x_ref.shape[1] // heads
    heads_chunk, pack = wide // size, 128 // size
    groups = read_ref.shape[1] // STATE
    ones = lambda mask: jnp.where(mask, 1.0, 0.0).astype(bf16)
    causal = iota((tokens, tokens), 0) >= iota((tokens, tokens), 1)
    lower, upper = ones(causal), ones(iota((tokens, tokens), 0) <= iota((tokens, tokens), 1))
    same = ones(iota((tokens, tokens), 0) == iota((tokens, tokens), 1))
    decays = split(decay_ref[...], 3)
    running = sum(dot(part, upper) for part in decays)
    running_t = sum(dot(lower, part, (1, 1)) for part in decays)
    step_t = sum(dot(same, part, (1, 1)) for part in split(step_ref[...], 3))
    runs[...] = running
    runs_t[...] = running_t
    ends_t[...] = jnp.exp(running_t[tokens - 1 : tokens, :] - running_t) * step_t
    grown_t[...] = jnp.exp(running_t)
    for g in range(groups):
        one = slice(g * STATE, (g + 1) * STATE)
        scores[g] = dot(read_ref[:, one], write_ref[:, one], (1, 1))

    def spread(value, k, width_head, parts):
        shape = (heads, heads_chunk * width_head)
        start = (iota(shape, 0) - k * heads_chunk) * width_head
        lane = iota(shape, 1)
        chosen = ones((lane >= start) & (lane < start + width_head))
        return sum(dot(part, chosen) for part in split(value, parts))

    def lanes(k):
        return pl.ds(pl.multiple_of(k * wide, wide), wide)

    def of_group(k):
        return pl.ds(pl.multiple_of(k // (chunks // groups) * STATE, STATE), STATE)

    def chain(k):
        return remote(cs.at[k], cr.at[k], csem.at[k], crem.at[k], seq=lax.rem(s + 1, ns))

    @pl.loop(0, chunks)
    def _(k):
        scaled = (x_ref[:, lanes(k)].astype(f32) * spread(ends_t[...], k, size, 2)).astype(bf16)
        local = dot(write_ref[:, of_group(k)], scaled, (0, 0))
        loc[k] = local
        drow[k] = spread(grown_t[tokens - 8 : tokens, :], k, size, 2)

        @pl.when(s == 0)
        def _():
            cr[k] = jnp.zeros(cr.shape[1:], bf16)
            cs[k] = local.astype(bf16)
            chain(k).start()

    def relay(k):
        chain(k).wait_recv()

        @pl.when(s < ns - 1)
        def _():
            cs[k] = (drow[k, 7:8, :] * cr[k].astype(f32) + loc[k]).astype(bf16)
            chain(k).start()

    @pl.when(s == 1)
    def _():
        @pl.loop(0, chunks)
        def _(k):
            relay(k)

    chosen_t = iota((tokens, probes), 0) == pos_ref[...]
    res_ref[...] = dot(ones(chosen_t), residual_ref[...], (0, 0)).astype(bf16)
    mixed_t = ones(chosen_t & (layer_ref[...] == 1))

    holds = h == s // ratio

    def residual(j):
        return remote(
            res_ref.at[:, j * width : (j + 1) * width], resbuf.at[block(s)], rs.at[j], rr.at[s], seq=h * ratio + j
        )

    def residual_from(src):
        return remote(res_ref.at[:, 0:width], resbuf.at[block(src)], rs.at[0], rr.at[src], seq=partner)

    for j in range(ratio):

        @pl.when(h * ratio + j != s)
        def _():
            residual(j).start()

        @pl.when(h * ratio + j == s)
        def _():
            resbuf[block(s), :] = res_ref[:, j * width : (j + 1) * width]

    @pl.loop(0, chunks)
    def _(k):
        gaps = spread(runs_t[...], k, tokens, 3)
        score = scores[k // (chunks // groups)]
        skips = spread(jnp.broadcast_to(skip_ref[...], (8, heads)), k, size, 3)[0:1, :]
        for pair in range(heads_chunk // pack):
            part = slice(pair * 128, (pair + 1) * 128)
            x = x_ref[:, pl.ds(pl.multiple_of(k * wide + pair * 128, 128), 128)]
            value = skips[:, part] * x.astype(f32)
            lane = iota(value.shape, 1)
            for one in range(pack):
                j = pair * pack + one
                head = pl.ds(k * heads_chunk + j, 1)
                gap = gaps[:, j * tokens : (j + 1) * tokens] - runs[head, :]
                weight = jnp.where(causal, jnp.exp(jnp.where(causal, gap, 0.0)), 0.0)
                weight = (weight * step_ref[head, :] * score).astype(bf16)
                mine = (lane >= one * size) & (lane < (one + 1) * size)
                value = value + jnp.where(mine, dot(weight, x), 0.0)
            wbuf[k, :, part] = value

    def direct(d, k):
        rows_of = gat.at[k, block(s)]
        return remote(rows_of, rows_of, gs.at[d, k], gr.at[d, k], seq=at_y(d) + c)

    def forward(d, k, core):
        rows_of = gat.at[k, block(at_y(-d) + core)]
        return remote(rows_of, rows_of, gs.at[ny - 1 + d, k], gr.at[ny - 1 + d, k], seq=partner)

    def to_partner(k):
        rows_of = gat.at[k, block(s)]
        return remote(rows_of, rows_of, gs.at[0, k], gr.at[0, k], seq=partner)

    @pl.loop(0, chunks)
    def _(k):
        @pl.when(s >= 2)
        def _():
            relay(k)

        across = dot(read_ref[:, of_group(k)], cr[k]) * spread(grown_t[...], k, size, 2)
        mixed = (wbuf[k] + across).astype(bf16)
        out_ref[:, lanes(k)] = mixed
        gat[k, block(s), :] = dot(mixed_t, mixed, (0, 0)).astype(bf16)
        for d in range(1, ny):
            direct(d, k).start()
        to_partner(k).start()

    proj_copy.wait()

    def arrive(k):
        for d in range(1, ny):
            direct(d, k).wait_recv()
            forward(d, k, c).start()
        to_partner(k).wait_recv()
        for d in range(1, ny):
            forward(d, k, 1 - c).wait_recv()

    @pl.loop(0, chunks - 1)
    def _(k):
        arrive(k)
        part = dot(gat[k], projv[pl.ds(pl.multiple_of(k * wide, wide), wide), :])

        @pl.when(k == 0)
        def _():
            prodf[...] = part

        @pl.when(k > 0)
        def _():
            prodf[...] += part

    arrive(chunks - 1)

    @pl.when(holds)
    def _():
        for d in range(1, ns):
            residual_from(lax.rem(s + d, ns)).wait_recv()

    sides = ((1, h, sright, rright, ssr_, srr_), (-1, nh - 1 - h, sleft, rleft, ssl, srl))

    def beside(step):
        return lax.rem(h + step + nh, nh)

    def passing(side, i):
        step, _, out, into, send, recv = side
        return remote(out.at[i], into.at[i], send.at[i], recv.at[i], head=beside(step))

    def columns(i):
        return pl.ds(pl.multiple_of(i * tile_w, tile_w), tile_w)

    near = jnp.minimum(h, nh - 1 - h)
    flying, lag = min(2, nct), 2

    @pl.loop(0, nct)
    def _(i):
        cols = columns(i)
        last = slice((chunks - 1) * wide, chunks * wide)
        part = dot(gat[chunks - 1], projv[last, cols])
        if chunks > 1:
            part = part + prodf[:, cols]
        prodf[:, cols] = part

        @pl.when(holds)
        def _():
            prodf[:, cols] += resbuf[:, cols].astype(f32)

        for side in sides:

            @pl.when(side[1] == 0)
            def _():
                side[2][i] = prodf[:, cols].astype(bf16)

                @pl.when(i >= flying)
                def _():
                    passing(side, i - flying).wait_send()

                passing(side, i).start()

    @pl.loop(0, nct + lag * (nh - 1))
    def _(j):
        for side in sides:
            i = j - lag * (side[1] - near)

            @pl.when((side[1] > 0) & (i >= 0) & (i < nct))
            def _():
                passing(side, i).wait_recv()

                @pl.when(side[1] < nh - 1)
                def _():
                    side[2][i] = (prodf[:, columns(i)] + side[3][i].astype(f32)).astype(bf16)
                    passing(side, i).start()

    order = [(core, d) for core in (0, 1) for d in range(ny)]

    def shard(core, d):
        return at_y(d) + (c if core == 0 else 1 - c)

    for i in range(nct):
        cols = slice(i * tile_w, (i + 1) * tile_w)
        gain = gain_ref[:, cols]
        for side in sides:

            @pl.when(side[1] > 0)
            def _():
                prodf[:, cols] += side[3][i].astype(f32)

        for k, (core, d) in enumerate(order):
            value = prodf[block(shard(core, d)), cols]
            lhs[k * probes : (k + 1) * probes, cols] = (value * gain).astype(bf16)
            squares = jnp.sum(value * value, axis=1, keepdims=True)
            squares = jnp.broadcast_to(squares, (probes, 128))
            if i > 0:
                squares = squares + ssb[shard(core, d)]
            ssb[shard(core, d)] = squares

    def send_squares(d):
        to = lax.rem(s + d, ns)
        return remote(ssb.at[to], ssr.at[d - 1], sqs.at[d - 1], sqr.at[d - 1], seq=to)

    for d in range(1, ns):
        send_squares(d).start()

    def to_core(t):
        return remote(sbuf.at[t], rbuf.at[t], as_.at[t], ar.at[t], seq=partner)

    def to_chip(t, d):
        return remote(s2b.at[t, d - 1], s2r.at[t, d - 1], bs.at[t, d - 1], br.at[t, d - 1], seq=at_y(d) + c)

    def second(t):
        to_core(t).wait_recv()
        value = kbuf[t] + rbuf[t].astype(f32)
        kbuf[t, 0:probes, :] = value[0:probes]
        for d in range(1, ny):
            s2b[t, d - 1] = value[d * probes : (d + 1) * probes].astype(bf16)
            to_chip(t, d).start()

    @pl.loop(0, tiles)
    def _(t):
        weights(t).wait()
        part = jnp.dot(lhs[...], wslots[lax.rem(t, slots)], preferred_element_type=f32)
        kbuf[t] = part[0:half]
        sbuf[t] = part[half:].astype(bf16)
        to_core(t).start()

        @pl.when(t + slots < tiles)
        def _():
            weights(t + slots).start()

        @pl.when(t > 0)
        def _():
            second(t - 1)

    second(tiles - 1)
    squares = ssb[s]
    for d in range(1, ns):
        send_squares(d).wait_recv()
        squares = squares + ssr[d - 1]
    inverse = lax.rsqrt(squares[:, 0:1] / (ns * width) + epsilon)

    def result(t):
        cols = pl.ds(pl.multiple_of(t * tile_v, tile_v), tile_v)
        return pltpu.make_async_copy(logits_ref.at[:, cols], logits_hbm.at[:, cols], osem.at[t])

    def finish(t, carry):
        high, total = carry
        value = kbuf[t, 0:probes, :]
        for d in range(1, ny):
            to_chip(t, d).wait_recv()
            value = value + s2r[t, d - 1].astype(f32)
        value = value * inverse
        logits_ref[:, pl.ds(pl.multiple_of(t * tile_v, tile_v), tile_v)] = value
        result(t).start()
        new = jnp.maximum(high, jnp.max(value, axis=1, keepdims=True))
        total = total * jnp.exp(high - new) + jnp.sum(jnp.exp(value - new), axis=1, keepdims=True)
        return new, total

    start = (jnp.full((probes, 1), -jnp.inf, f32), jnp.zeros((probes, 1), f32))
    high, total = lax.fori_loop(0, tiles, finish, start)
    stats[0] = jnp.broadcast_to(high, (probes, 128))
    stats[1] = jnp.broadcast_to(total, (probes, 128))

    def send_stats(d):
        return remote(stats, statr.at[d - 1], hs.at[d - 1], hr.at[d - 1], head=lax.rem(h + d, nh))

    for d in range(1, nh):
        send_stats(d).start()

    @pl.loop(0, chunks)
    def _(k):
        @pl.when(s < ns - 1)
        def _():
            chain(k).wait_send()

        for d in range(1, ny):
            direct(d, k).wait_send()
            forward(d, k, c).wait_send()
        to_partner(k).wait_send()

    for j in range(ratio):

        @pl.when(h * ratio + j != s)
        def _():
            residual(j).wait_send()

    for d in range(1, ns):
        send_squares(d).wait_send()

    @pl.loop(0, nct)
    def _(i):
        for side in sides:

            @pl.when((side[1] < nh - 1) & ((side[1] > 0) | (i >= nct - flying)))
            def _():
                passing(side, i).wait_send()

    @pl.loop(0, tiles)
    def _(t):
        to_core(t).wait_send()
        result(t).wait()
        for d in range(1, ny):
            to_chip(t, d).wait_send()

    for d in range(1, nh):
        send_stats(d).wait_recv()
    highest = stats[0]
    for d in range(1, nh):
        highest = jnp.maximum(highest, statr[d - 1, 0])
    merged = stats[1] * jnp.exp(stats[0] - highest)
    for d in range(1, nh):
        merged = merged + statr[d - 1, 1] * jnp.exp(statr[d - 1, 0] - highest)
    lse_ref[...] = highest + jnp.log(merged)

    for d in range(1, nh):
        send_stats(d).wait_send()


def fused(ns, nh, x, write, read, decay, step, skip, residual, position, layer, gain, out_proj, lens_weight):
    probes, (tokens, inner), heads = position.shape[1], x.shape, decay.shape[0]
    chunks = max(inner // 512, 1)
    wide = inner // chunks
    width, vocab = lens_weight.shape
    rows, ny = ns * probes, ns // 2
    tile_w, tile_v = min(256, width), min(1024, vocab)
    nct, tiles = width // tile_w, vocab // tile_v
    slots = min(4, tiles)
    half = ny * probes
    dma = pltpu.SemaphoreType.DMA
    more = max(ny - 1, 1)
    return pl.pallas_call(
        partial(lens_kernel, ns, nh),
        out_shape=(
            jax.ShapeDtypeStruct((tokens, inner), bf16),
            jax.ShapeDtypeStruct((probes, vocab), f32),
            jax.ShapeDtypeStruct((probes, 128), f32),
        ),
        in_specs=[ANY] * 3 + [VMEM] * 3 + [ANY] + [VMEM] * 3 + [ANY, ANY],
        out_specs=(VMEM, ANY, VMEM),
        scratch_shapes=[
            pltpu.VMEM(x.shape, bf16),
            pltpu.VMEM(write.shape, bf16),
            pltpu.VMEM(read.shape, bf16),
            pltpu.VMEM(residual.shape, bf16),
            dma((4,)),
            pltpu.VMEM((probes, vocab), f32),
            dma((tiles,)),
            pltpu.VMEM((heads, tokens), f32),
            pltpu.VMEM((tokens, heads), f32),
            pltpu.VMEM((tokens, heads), f32),
            pltpu.VMEM((tokens, heads), f32),
            pltpu.VMEM((read.shape[1] // STATE, tokens, tokens), f32),
            pltpu.VMEM((chunks, STATE, wide), f32),
            pltpu.VMEM((chunks, tokens, wide), f32),
            pltpu.VMEM((chunks, 8, wide), f32),
            pltpu.VMEM((chunks, STATE, wide), bf16),
            pltpu.VMEM((chunks, STATE, wide), bf16),
            pltpu.VMEM((probes, residual.shape[1]), bf16),
            pltpu.VMEM((chunks, rows, wide), bf16),
            pltpu.VMEM((rows, width), bf16),
            pltpu.VMEM((inner, width), bf16),
            pltpu.VMEM((slots, width, tile_v), bf16),
            pltpu.VMEM((rows, width), f32),
            pltpu.VMEM((nct, rows, tile_w), bf16),
            pltpu.VMEM((nct, rows, tile_w), bf16),
            pltpu.VMEM((nct, rows, tile_w), bf16),
            pltpu.VMEM((nct, rows, tile_w), bf16),
            pltpu.VMEM((rows, width), bf16),
            pltpu.VMEM((ns, probes, 128), f32),
            pltpu.VMEM((ns - 1, probes, 128), f32),
            pltpu.VMEM((tiles, half, tile_v), f32),
            pltpu.VMEM((tiles, half, tile_v), bf16),
            pltpu.VMEM((tiles, half, tile_v), bf16),
            pltpu.VMEM((tiles, more, probes, tile_v), bf16),
            pltpu.VMEM((tiles, more, probes, tile_v), bf16),
            pltpu.VMEM((2, probes, 128), f32),
            pltpu.VMEM((nh - 1, 2, probes, 128), f32),
            dma((chunks,)),
            dma((chunks,)),
            dma((slots,)),
            dma,
            dma((ns - 1, chunks)),
            dma((ns - 1, chunks)),
            dma((ns // nh,)),
            dma((ns,)),
            dma((nct,)),
            dma((nct,)),
            dma((nct,)),
            dma((nct,)),
            dma((ns - 1,)),
            dma((ns - 1,)),
            dma((tiles,)),
            dma((tiles,)),
            dma((tiles, more)),
            dma((tiles, more)),
            dma((nh - 1,)),
            dma((nh - 1,)),
        ],
        compiler_params=pltpu.CompilerParams(
            collective_id=0, has_side_effects=True, vmem_limit_bytes=67043328
        ),
    )(x, write, read, decay, step, skip, residual, position, layer, gain, out_proj, lens_weight)


def result_kernel(mixed_hbm, logits_hbm, lse_ref, out_hbm, logprobs_hbm, buffer, mixed, isem, osem, msem):
    rows, vocab = logits_hbm.shape
    parts = isem.shape[0]
    size = vocab // parts
    steps = mixed.shape[0] // 4
    cols = [slice(i * size, (i + 1) * size) for i in range(parts)]
    some = [slice(i * steps, (i + 1) * steps) for i in range(4)]
    mixed_in = [pltpu.make_async_copy(mixed_hbm.at[r], mixed.at[r], msem.at[0, i]) for i, r in enumerate(some)]
    mixed_out = [pltpu.make_async_copy(mixed.at[r], out_hbm.at[r], msem.at[1, i]) for i, r in enumerate(some)]
    take = [pltpu.make_async_copy(logits_hbm.at[:, c], buffer.at[:, c], isem.at[i]) for i, c in enumerate(cols)]
    give = [pltpu.make_async_copy(buffer.at[:, c], logprobs_hbm.at[:, c], osem.at[i]) for i, c in enumerate(cols)]
    for copy in mixed_in + take:
        copy.start()
    for first, then in zip(mixed_in, mixed_out):
        first.wait()
        then.start()
    lse = lse_ref[:, 0:1]
    for i, c in enumerate(cols):
        take[i].wait()
        buffer[:, c] = buffer[:, c] - lse
        give[i].start()
    for copy in mixed_out + give:
        copy.wait()


def finished(mixed, logits, lse):
    dma = pltpu.SemaphoreType.DMA
    parts = 8
    return pl.pallas_call(
        result_kernel,
        out_shape=(jax.ShapeDtypeStruct(mixed.shape, bf16), jax.ShapeDtypeStruct(logits.shape, f32)),
        in_specs=[ANY, ANY, VMEM],
        out_specs=(ANY, ANY),
        scratch_shapes=[
            pltpu.VMEM(logits.shape, f32),
            pltpu.VMEM(mixed.shape, bf16),
            dma((parts,)),
            dma((parts,)),
            dma((2, 4)),
        ],
        compiler_params=pltpu.CompilerParams(vmem_limit_bytes=67043328),
    )(mixed, logits, lse)


def per_device(
    mixer_input,
    state_input,
    state_output,
    log_decay,
    step_size,
    skip_gain,
    residual,
    out_proj,
    norm_gain,
    lens_weight,
    probe_position,
    probe_layer,
):
    ns, nh = lax.axis_size("seq"), lax.axis_size("head")
    mixed, logits, lse = fused(
        ns,
        nh,
        mixer_input,
        state_input,
        state_output,
        log_decay,
        step_size,
        skip_gain[None, :],
        residual,
        probe_position[None, :],
        probe_layer[None, :],
        norm_gain[None, :],
        out_proj,
        lens_weight,
    )
    return finished(mixed, logits, lse)


def solution(mesh):
    return jax.shard_map(
        per_device,
        mesh=mesh,
        in_specs=(
            P(("groups", "seq"), "head"),
            P(("groups", "seq"), "head"),
            P(("groups", "seq"), "head"),
            P("head", ("groups", "seq")),
            P("head", ("groups", "seq")),
            P("head"),
            P(("groups", "seq"), "head"),
            P("head", "seq"),
            P("seq"),
            P("seq", "head"),
            P(("groups", "seq")),
            P(("groups", "seq")),
        ),
        out_specs=(P(("groups", "seq"), "head"), P(("groups", "seq"), "head")),
        check_vma=False,
    )
```
